32 devices in a mesh: wide: 8 (over z, y), orb: 4 (over x, core).
Axes of the slice: x: 2, y: 2, z: 4, core: 2. Of those that a mesh axis runs over, the one named last changes fastest.
Arguments:
- green_packed: bfloat16 [2, 8, 16, 256, 256], P(None, 'wide', 'orb'), may hold values from -6 to 6
- bubble_weight: float32 [16, 16], replicated, may hold values from -1.5 to 1.5
- tile_owner: int32 [64], replicated, may hold values from 0 to 63, as said below
- pairing: int32 [64], replicated, may hold values from 0 to 63, as said below
Outputs:
- response: bfloat16 [2, 8, 16, 256, 256], P(None, 'wide', 'orb')
The draws below stay inside these ranges and needn't reach their ends.
Inputs may be any that keep to these rules, and one draw needn't show every extreme that they name: `tile_owner`: A permutation of the 64 time tiles; slot s lies on index s // (8 * 8 / 8) of wide. The tiles in slots s and s + 32 are mirror images (tiles i * 8 + j and j * 8 + i) or both diagonal tiles. pairing[s] is the slot whose tile is the mirror image of tile_owner[s]: s itself for a diagonal tile, else the slot 32 away.
All inputs are finite; a program needn't handle non-finite values.
Results may differ from the reference program's by a relative error of at most 0.018.
Values may be sent and summed in bfloat16 or wider, within the bound.
No kernel may reach another device: no remote copies, remote signals or barrier semaphores. Data moves between devices by JAX's collectives and lax.ppermute only.
A program may use at most 128 MiB of HBM per device.

```python
import jax
import jax.numpy as jnp
import numpy as np
from jax import lax

NORB = 4
NP = 16
K = 8
NT = 256
NTILE = 8
TS = 32


def mirror_units():
    leading = []
    trailing = []
    for upper_row in range(NTILE):
        for lower_row in range(upper_row + 1, NTILE):
            leading.append(upper_row * NTILE + lower_row)
            trailing.append(lower_row * NTILE + upper_row)
    for middle in range(NTILE // 2):
        leading.append(2 * middle * (NTILE + 1))
        trailing.append((2 * middle + 1) * (NTILE + 1))
    return (np.array(leading, np.int32), np.array(trailing, np.int32))


def slot_tables(key):
    leading, trailing = mirror_units()
    half_count = NTILE * NTILE // 2
    shuffled = jax.random.permutation(jax.random.fold_in(key, 71), half_count)
    flipped = jax.random.randint(jax.random.fold_in(key, 72), (half_count,), 0, 2)
    lead_tiles = jnp.asarray(leading)[shuffled]
    trail_tiles = jnp.asarray(trailing)[shuffled]
    upper_half = jnp.where(flipped == 1, trail_tiles, lead_tiles)
    lower_half = jnp.where(flipped == 1, lead_tiles, trail_tiles)
    owners = jnp.concatenate([upper_half, lower_half]).astype(jnp.int32)
    slot_ids = jnp.arange(2 * half_count, dtype=jnp.int32)
    diagonal = owners // NTILE == owners % NTILE
    partner = jnp.where(diagonal, slot_ids, (slot_ids + half_count) % (2 * half_count))
    return (owners, partner.astype(jnp.int32))


def draw_tile_owner(key, part):
    return slot_tables(key)[0]


def draw_pairing(key, part):
    return slot_tables(key)[1]


def levels(key, shape, split, low, high):
    gain, own = 1.0, jax.random.fold_in(key, 6)
    for dim, blocks in split:
        heights = jnp.exp(jax.random.uniform(jax.random.fold_in(own, dim), (blocks,), jnp.float32, low / len(split), high / len(split)))
        gain = gain * jnp.repeat(heights, shape[dim] // blocks).reshape([-1 if axis == dim else 1 for axis in range(len(shape))])
    return gain


def gaussian(stream_key, dims, scale, reach, split=(), held_as=jnp.bfloat16):
    values = scale * jax.random.normal(stream_key, dims, jnp.float32)
    if split:
        values = values * levels(stream_key, dims, split, -0.22, 0.18)
    return jnp.clip(values, -reach, reach).astype(held_as)


def setup_inputs(seed: int = 0) -> dict:
    key_of = jax.random.split(jax.random.key(seed), 5)
    return {
        "green_packed": gaussian(key_of[0], (2, K, NP, NT, NT), 1.0, 6.0, ((1, 8), (2, 4))),
        "bubble_weight": gaussian(key_of[1], (NP, NP), NP ** -0.5, 1.5, (), jnp.float32),
        "tile_owner": draw_tile_owner(jax.random.fold_in(key_of[4], 71), 0),
        "pairing": draw_pairing(jax.random.fold_in(key_of[4], 71), 0),
    }


precise = lax.Precision.HIGHEST


def complex_mix(former, latter):
    def single(first_op, second_op):
        return jnp.einsum("acts,cbsu->abtu", first_op, second_op, precision=precise)
    real_part = single(former[0], latter[0]) - single(former[1], latter[1])
    imag_part = single(former[0], latter[1]) + single(former[1], latter[0])
    return jnp.stack([real_part, imag_part], axis=0)


def reference(green_packed, bubble_weight, tile_owner, pairing):
    tile_area = TS * TS
    blocks = green_packed.reshape(2, K, NP, NTILE, TS, NTILE, TS).transpose(3, 5, 0, 1, 2, 4, 6)
    blocks = blocks.reshape(NTILE * NTILE, 2, K, NP, tile_area)
    group_weight = bubble_weight.astype(jnp.float32).reshape(NP, NORB, NORB)

    def to_real(tile_data):
        values = tile_data.astype(jnp.float32)
        spread = jnp.fft.ifft(lax.complex(values[0], values[1]), axis=0, norm="ortho")
        return jnp.stack([jnp.real(spread), jnp.imag(spread)], axis=0).astype(jnp.bfloat16)

    def slot_self(slot):
        own_tile = lax.dynamic_index_in_dim(blocks, tile_owner[slot].astype(jnp.int32), 0, keepdims=False)
        other_slot = pairing[slot].astype(jnp.int32)
        other_tile = lax.dynamic_index_in_dim(blocks, tile_owner[other_slot].astype(jnp.int32), 0, keepdims=False)
        real_green = to_real(own_tile)
        facing = to_real(other_tile)
        extent = facing.shape
        facing = jnp.swapaxes(facing.reshape(extent[:-1] + (TS, TS)), -1, -2).reshape(extent)
        mirror = jnp.roll(jnp.flip(facing, axis=1), 1, axis=1)
        own32 = real_green.astype(jnp.float32)
        mirror32 = mirror.astype(jnp.float32)
        product = jnp.stack([own32[0] * mirror32[0] - own32[1] * mirror32[1],
                             own32[0] * mirror32[1] + own32[1] * mirror32[0]], axis=0)
        grouped = product.reshape(2, K, NORB, NORB, tile_area)
        partial_value = jnp.einsum("qab,ckabx->ackqx", group_weight, grouped, precision=precise)
        partial_value = lax.optimization_barrier(partial_value.astype(jnp.bfloat16)).astype(jnp.float32)
        bubble = jnp.sum(partial_value, axis=0)
        self_re = own32[0] * bubble[0] - own32[1] * bubble[1]
        self_im = own32[0] * bubble[1] + own32[1] * bubble[0]
        back = jnp.fft.fft(lax.complex(self_re, self_im), axis=0, norm="ortho")
        return jnp.stack([jnp.real(back), jnp.imag(back)], axis=0).astype(jnp.bfloat16)

    self_slots = lax.map(slot_self, jnp.arange(NTILE * NTILE, dtype=jnp.int32))
    placed = jnp.zeros_like(self_slots).at[tile_owner].set(self_slots)
    self_energy = placed.reshape(NTILE, NTILE, 2, K, NP, TS, TS).transpose(2, 3, 4, 0, 5, 1, 6)
    self_energy = self_energy.reshape(2, K, NP, NT, NT)

    positions = jnp.arange(NT, dtype=jnp.int32)
    lower_mask = positions[:, None] >= positions[None, :]
    strict_lower = positions[:, None] > positions[None, :]
    conj_sign = jnp.array([1.0, -1.0], jnp.float32).reshape(2, 1, 1, 1, 1)

    def per_momentum(pieces):
        green_k, self_k = pieces
        green32 = green_k.astype(jnp.float32).reshape(2, NORB, NORB, NT, NT)
        self32 = self_k.astype(jnp.float32).reshape(2, NORB, NORB, NT, NT)
        swapped = green32.transpose(0, 2, 1, 4, 3)
        retarded_g = jnp.where(lower_mask, green32, 0.0)
        lesser_g = jnp.where(lower_mask, jnp.where(strict_lower, -conj_sign * swapped, 0.0), green32)
        advanced_g = jnp.where(strict_lower, 0.0, conj_sign * swapped)
        retarded_s = jnp.where(lower_mask, self32, 0.0)
        upper_s = jnp.where(lower_mask, 0.0, self32)
        retarded = complex_mix(retarded_s, retarded_g)
        lesser = complex_mix(retarded_s, lesser_g) + complex_mix(upper_s, advanced_g)
        combined = jnp.where(lower_mask, retarded, lesser) * (NT ** -0.5)
        return combined.reshape(2, NP, NT, NT).astype(jnp.bfloat16)

    response = lax.map(per_momentum, (jnp.moveaxis(green_packed, 1, 0), jnp.moveaxis(self_energy, 1, 0)))
    return jnp.moveaxis(response, 0, 1)
```

```python
import functools
import math

import jax
import jax.numpy as jnp
from jax import lax
from jax.experimental import pallas as pl
from jax.experimental.pallas import tpu as pltpu
from jax.sharding import PartitionSpec as P


F32 = jnp.float32
BF16 = jnp.bfloat16
VMEM = pl.BlockSpec(memory_space=pltpu.VMEM)
SMEM = pl.BlockSpec(memory_space=pltpu.SMEM)
PARAMS = pltpu.CompilerParams(vmem_limit_bytes=56 * 1024 * 1024)


def grid_masks(half):
    rows = lax.broadcasted_iota(jnp.int32, (half, half), 0)
    cols = lax.broadcasted_iota(jnp.int32, (half, half), 1)
    return rows, cols


def pack_kernel(green_ref, out_ref):
    count, momenta, _, pairs, _, rows, half = out_ref.shape
    row, col = grid_masks(half)

    def one(step, carry):
        part, pair = step // pairs, step % pairs
        for k in range(momenta):
            def block(i, j):
                return green_ref[part, k, pair, i * half : (i + 1) * half, j * half : (j + 1) * half].astype(F32)

            b00, b11 = block(0, 0), block(1, 1)
            own = jnp.concatenate([block(0, 1), jnp.where(row >= col, b00, b11)], 0)
            facing = jnp.concatenate([block(1, 0).T, jnp.where(row < col, b00, b11).T], 0)
            out_ref[:, k, part, pair, 0] = own.reshape(count, rows, half).astype(BF16)
            out_ref[:, k, part, pair, 1] = facing.reshape(count, rows, half).astype(BF16)
        return carry

    lax.fori_loop(0, 2 * pairs, one, 0)


def twiddle(re, im, angle):
    cos, sin = math.cos(angle), math.sin(angle)
    if abs(sin) < 1e-12:
        return (re, im) if cos > 0 else (-re, -im)
    if abs(cos) < 1e-12:
        return (-im, re) if sin > 0 else (im, -re)
    return re * cos - im * sin, re * sin + im * cos


def dft(values, sign):
    size = len(values)
    if size == 1:
        return values
    out = [None] * size
    if size % 2:
        for r in range(size):
            terms = [twiddle(*values[k], sign * 2 * math.pi * (k * r % size) / size) for k in range(size)]
            out[r] = (sum(t[0] for t in terms), sum(t[1] for t in terms))
        return out
    even, odd = dft(values[0::2], sign), dft(values[1::2], sign)
    for r in range(size // 2):
        re, im = twiddle(*odd[r], sign * 2 * math.pi * r / size)
        out[r] = (even[r][0] + re, even[r][1] + im)
        out[r + size // 2] = (even[r][0] - re, even[r][1] - im)
    return out


def middle_kernel(device_ref, weight_ref, in_ref, out_ref, real_scr, product_scr):
    count, per_device, _, pairs, _, rows, half = in_ref.shape
    all_pairs = weight_ref.shape[0] // rows
    orbs = all_pairs // pairs
    wide = count // orbs
    momenta = wide * per_device
    factor = momenta ** -0.5
    spot = lax.broadcasted_iota(jnp.int32, (rows, half), 0) + (device_ref[0] * rows - half)
    diagonal = spot == lax.broadcasted_iota(jnp.int32, (rows, half), 1)

    def lanes(sheet, part, r):
        return pl.ds(((sheet * 2 + part) * momenta + r) * half, half)

    def forward(pair, carry):
        orb, local = pair // pairs, pair % pairs
        real = []
        for sheet in range(2):
            values = [
                tuple(in_ref[w * orbs + orb, k, part, local, sheet].astype(F32) * factor for part in range(2))
                for w in range(wide)
                for k in range(per_device)
            ]
            real.append(dft(values, 1.0))
        for sheet in range(2):
            for r in range(momenta):
                re, im = real[sheet][r]
                real_scr[pair, :, lanes(sheet, 0, r)] = re
                real_scr[pair, :, lanes(sheet, 1, r)] = im
                back = -r % momenta
                mre, mim = (
                    jnp.where(diagonal, real[sheet][back][part], real[1 - sheet][back][part]) for part in range(2)
                )
                product_scr[pair, :, lanes(sheet, 0, r)] = re * mre - im * mim
                product_scr[pair, :, lanes(sheet, 1, r)] = re * mim + im * mre
        return carry

    lax.fori_loop(0, all_pairs, forward, 0)
    product = product_scr[...].reshape(all_pairs * rows, -1).astype(BF16)
    bubble = jnp.dot(weight_ref[...], product, preferred_element_type=F32)
    product_scr[...] = bubble.reshape(product_scr.shape)

    def backward(pair, carry):
        orb, local = pair // pairs, pair % pairs
        for sheet in range(2):
            values = []
            for r in range(momenta):
                re, im = (real_scr[pair, :, lanes(sheet, part, r)] for part in range(2))
                bre, bim = (product_scr[pair, :, lanes(sheet, part, r)] * factor for part in range(2))
                values.append((re * bre - im * bim, re * bim + im * bre))
            values = dft(values, -1.0)
            for w in range(wide):
                for k in range(per_device):
                    for part in range(2):
                        out_ref[w * orbs + orb, k, part, local, sheet] = values[w * per_device + k][part].astype(BF16)
        return carry

    lax.fori_loop(0, all_pairs, backward, 0)


def langreth_kernel(orb_ref, self_ref, *refs):
    orbs = self_ref.shape[3]
    green_refs, out_ref, lhs_scr, tile_scr = refs[:orbs], refs[orbs], refs[orbs + 1], refs[orbs + 2]
    count, momenta, _, _, _, rows, half = self_ref.shape
    me = orb_ref[0]
    row, col = grid_masks(half)
    zero = jnp.zeros((half, half), F32)
    scale = (2 * half) ** -0.5
    for k in range(momenta):
        for turn in range(orbs):
            c = me ^ turn
            for part in range(2):
                def sheet(index, lower):
                    span = slice(count // 2, count) if lower else slice(0, count // 2)
                    return self_ref[span, k, part, c, index].astype(F32).reshape(half, half)

                own, facing = sheet(0, True), sheet(1, True).T
                pieces = [
                    jnp.where(row >= col, own, zero),
                    sheet(1, False).T,
                    jnp.where(row >= col, facing, zero),
                    jnp.where(row < col, facing, zero),
                    sheet(0, False),
                    jnp.where(row < col, own, zero),
                ]
                for n, piece in enumerate(pieces):
                    lhs_scr[n * half : (n + 1) * half, (2 * turn + part) * half : (2 * turn + part + 1) * half] = piece.astype(BF16)

            def tiles(local, carry):
                blocks = {}
                for part in range(2):
                    for i in range(2):
                        for j in range(2):
                            blocks[part, i, j] = green_refs[turn][
                                part, k, local, i * half : (i + 1) * half, j * half : (j + 1) * half
                            ].astype(F32)
                picks = [
                    [jnp.where(row >= col, blocks[part, 0, 0], zero) for part in range(2)],
                    [blocks[part, 1, 0] for part in range(2)],
                    [jnp.where(row >= col, blocks[part, 1, 1], zero) for part in range(2)],
                    [jnp.where(row < col, blocks[part, 0, 0], zero) for part in range(2)],
                    [blocks[part, 0, 1] for part in range(2)],
                    [jnp.where(row < col, blocks[part, 1, 1], zero) for part in range(2)],
                ]
                for n, (re, im) in enumerate(picks):
                    tile_scr[turn, local, n, :half, :half] = re.astype(BF16)
                    tile_scr[turn, local, n, :half, half:] = im.astype(BF16)
                    tile_scr[turn, local, n, half:, :half] = (-im).astype(BF16)
                    tile_scr[turn, local, n, half:, half:] = re.astype(BF16)
                return carry

            lax.fori_loop(0, orbs, tiles, 0)

        def target(turn_b, carry):
            b = me ^ turn_b

            def left(first, last):
                return lhs_scr[first * half : last * half, :]

            def plain(lhs, n):
                rhs = jnp.concatenate([tile_scr[turn, b, n] for turn in range(orbs)], 0)
                return jnp.dot(lhs, rhs, preferred_element_type=F32)

            def adjoint(lhs, n):
                rhs = jnp.concatenate([tile_scr[turn_b, me ^ turn, n] for turn in range(orbs)], 1)
                return lax.dot_general(lhs, rhs, (((1,), (1,)), ((), ())), preferred_element_type=F32)

            upper = left(0, 2)
            d1 = plain(upper, 0)
            d2 = plain(upper, 4)
            d9 = adjoint(left(4, 6), 2)
            low = left(2, 3)
            back = left(3, 4)
            out10 = d1[half:] + plain(low, 1)
            out01 = d2[:half] + d9[:half] + adjoint(back, 1)
            ret00, ret11 = d1[:half], plain(low, 2)
            les00 = plain(left(0, 1), 3) + adjoint(back, 0)
            les11 = d2[half:] + d9[half:] + plain(low, 5)
            for part in range(2):
                at = slice(part * half, (part + 1) * half)
                out_ref[part, k, b, :half, :half] = (jnp.where(row >= col, ret00[:, at], les00[:, at]) * scale).astype(BF16)
                out_ref[part, k, b, half:, half:] = (jnp.where(row >= col, ret11[:, at], les11[:, at]) * scale).astype(BF16)
                out_ref[part, k, b, :half, half:] = (out01[:, at] * scale).astype(BF16)
                out_ref[part, k, b, half:, :half] = (out10[:, at] * scale).astype(BF16)
            return carry

        lax.fori_loop(0, orbs, target, 0)


def local(wide, orbs, green, bubble_weight, tile_owner, pairing):
    parts, momenta, pairs, times, _ = green.shape
    all_pairs = bubble_weight.shape[0]
    half = times // 2
    count = wide * orbs
    rows = times // count
    axes = ("wide", "orb")
    sheet_shape = (count, momenta, parts, pairs, 2, rows, half)
    sheets = jax.ShapeDtypeStruct(sheet_shape, BF16)
    device = lax.axis_index(axes).astype(jnp.int32).reshape(1)
    orb = lax.axis_index("orb").astype(jnp.int32).reshape(1)

    packed = pl.pallas_call(
        pack_kernel, out_shape=sheets, in_specs=[VMEM], out_specs=VMEM, compiler_params=PARAMS, name="pack"
    )(green)

    greens = {0: green}
    bit = orbs // 2
    while bit:
        swap = [(i, i ^ bit) for i in range(orbs)]
        greens.update({turn ^ bit: lax.ppermute(piece, "orb", swap) for turn, piece in greens.items()})
        bit //= 2
    greens = [greens[turn] for turn in range(orbs)]

    arrived = lax.all_to_all(packed, axes, 0, 0, tiled=True)
    spread = jnp.kron(bubble_weight, jnp.eye(rows, dtype=F32)).astype(BF16)
    width = 2 * parts * momenta * wide * half
    sent = pl.pallas_call(
        middle_kernel,
        out_shape=sheets,
        in_specs=[SMEM, VMEM, VMEM],
        out_specs=VMEM,
        scratch_shapes=[pltpu.VMEM((all_pairs, rows, width), F32)] * 2,
        compiler_params=PARAMS,
        name="middle",
    )(device, spread, arrived)
    returned = lax.all_to_all(sent, axes, 0, 0, tiled=True)

    return pl.pallas_call(
        langreth_kernel,
        out_shape=jax.ShapeDtypeStruct(green.shape, BF16),
        in_specs=[SMEM, VMEM] + [VMEM] * orbs,
        out_specs=VMEM,
        scratch_shapes=[
            pltpu.VMEM((6 * half, 2 * orbs * half), BF16),
            pltpu.VMEM((orbs, orbs, 6, 2 * half, 2 * half), BF16),
        ],
        compiler_params=PARAMS,
        name="langreth",
    )(orb, returned, *greens)


def solution(mesh):
    return jax.shard_map(
        functools.partial(local, mesh.shape["wide"], mesh.shape["orb"]),
        mesh=mesh,
        in_specs=(P(None, "wide", "orb", None, None), P(), P(), P()),
        out_specs=P(None, "wide", "orb", None, None),
        check_vma=False,
    )
```

```python
import functools
import math

import jax
import jax.numpy as jnp
from jax import lax
from jax.experimental import pallas as pl
from jax.experimental.pallas import tpu as pltpu
from jax.sharding import PartitionSpec as P


F32 = jnp.float32
BF16 = jnp.bfloat16
VMEM = pl.BlockSpec(memory_space=pltpu.VMEM)
SMEM = pl.BlockSpec(memory_space=pltpu.SMEM)
HBM = pl.BlockSpec(memory_space=pltpu.HBM)


def limit(mebibytes):
    return pltpu.CompilerParams(vmem_limit_bytes=mebibytes * 1024 * 1024)


def grid_masks(half):
    rows = lax.broadcasted_iota(jnp.int32, (half, half), 0)
    cols = lax.broadcasted_iota(jnp.int32, (half, half), 1)
    return rows, cols


def places(count, near, sent):
    if sent:
        return [(rel // near, (rel % 2, rel % near // 2)) for rel in range(count)]
    return [(rel % near // 2, (rel % 2, rel // near)) for rel in range(count)]


def emit(block_scr, me, out_refs, spots):
    if spots is None:
        out_refs[0][...] = block_scr[...]
        return
    for rel, (n, at) in enumerate(spots):
        out_refs[n].at[at][...] = block_scr[me ^ rel]


def collect(block_scr, me, in_refs, spots):
    if spots is None:
        block_scr[...] = in_refs[0][...]
        return
    for rel, (n, at) in enumerate(spots):
        block_scr[me ^ rel] = in_refs[n].at[at][...]


def entries(spots):
    return 1 if spots is None else 1 + max(n for n, _ in spots)


def halves(own, facing, count):
    rows = own.shape[0] // count
    return [
        jnp.concatenate([own[d * rows : (d + 1) * rows], facing[d * rows : (d + 1) * rows]], 0)
        for d in range(count)
    ]


def pack_kernel(blocks, spots, device_ref, green_ref, *refs):
    raw_ref, out_refs, block_scr, green_scr, sems = refs[0], refs[1:-3], refs[-3], refs[-2], refs[-1]
    count, momenta, parts, pairs, _, half = block_scr.shape
    row, col = grid_masks(half)

    def fetch(step, target=green_scr, kind=0):
        part, pair = step // pairs, step % pairs
        return [
            pltpu.make_async_copy(
                green_ref.at[part, :, pair, pl.ds(i * half, half), pl.ds(j * half, half)],
                target.at[step, n],
                sems.at[kind, step, n],
            )
            for n, (i, j) in enumerate(blocks)
        ]

    def begin(step, carry):
        for copy in fetch(step) + fetch(step, raw_ref, 1):
            copy.start()
        return carry

    lax.fori_loop(0, parts * pairs, begin, 0)

    def one(step, carry):
        part, pair = step // pairs, step % pairs
        for copy in fetch(step):
            copy.wait()
        for k in range(momenta):
            got = {at: green_scr[step, n, k].astype(F32) for n, at in enumerate(blocks)}
            own, facing = [], []
            if (0, 1) in got:
                own.append(got[0, 1])
                facing.append(got[1, 0].T)
            if (0, 0) in got:
                own.append(jnp.where(row >= col, got[0, 0], got[1, 1]))
                facing.append(jnp.where(row < col, got[0, 0], got[1, 1]).T)
            own, facing = (jnp.concatenate(x, 0) if len(x) > 1 else x[0] for x in (own, facing))
            for d, piece in enumerate(halves(own, facing, count)):
                block_scr[d, k, part, pair] = piece.astype(BF16)
        return carry

    lax.fori_loop(0, parts * pairs, one, 0)
    emit(block_scr, device_ref[0], out_refs, spots)

    def finish(step, carry):
        for copy in fetch(step, raw_ref, 1):
            copy.wait()
        return carry

    lax.fori_loop(0, parts * pairs, finish, 0)


def twiddle(re, im, angle):
    cos, sin = math.cos(angle), math.sin(angle)
    if abs(sin) < 1e-12:
        return (re, im) if cos > 0 else (-re, -im)
    if abs(cos) < 1e-12:
        return (-im, re) if sin > 0 else (im, -re)
    return re * cos - im * sin, re * sin + im * cos


def dft(values, sign):
    size = len(values)
    if size == 1:
        return values
    out = [None] * size
    if size % 2:
        for r in range(size):
            terms = [twiddle(*values[k], sign * 2 * math.pi * (k * r % size) / size) for k in range(size)]
            out[r] = (sum(t[0] for t in terms), sum(t[1] for t in terms))
        return out
    even, odd = dft(values[0::2], sign), dft(values[1::2], sign)
    for r in range(size // 2):
        re, im = twiddle(*odd[r], sign * 2 * math.pi * r / size)
        out[r] = (even[r][0] + re, even[r][1] + im)
        out[r + size // 2] = (even[r][0] - re, even[r][1] - im)
    return out


def middle_kernel(start, came_spots, sent_spots, device_ref, weight_ref, *refs):
    real_scr, product_scr, block_scr = refs[-3:]
    count, per_device, _, pairs, rows2, half = block_scr.shape
    all_pairs = weight_ref.shape[0] // rows2
    orbs = all_pairs // pairs
    wide = count // orbs
    momenta = wide * per_device
    factor = momenta ** -0.5
    me = device_ref[0]
    inputs = entries(came_spots)
    in_refs, out_refs = refs[:inputs], refs[inputs:-3]
    rows = rows2 // 2
    if start is not None:
        spot = lax.broadcasted_iota(jnp.int32, (rows2, half), 0)
        spot = jnp.where(spot >= rows, spot - rows, spot) + (me * rows + start)
        diagonal = spot == lax.broadcasted_iota(jnp.int32, (rows2, half), 1)

    collect(block_scr, me, in_refs, came_spots)

    def lanes(part, r):
        return pl.ds((part * momenta + r) * half, half)

    def across(x):
        if rows2 == 8:
            return pltpu.roll(x, rows, 0)
        return jnp.concatenate([x[rows:], x[:rows]], 0)

    def forward(pair, carry):
        orb, local = pair // pairs, pair % pairs
        values = [
            tuple(block_scr[w * orbs + orb, k, part, local].astype(F32) * factor for part in range(2))
            for w in range(wide)
            for k in range(per_device)
        ]
        real = dft(values, 1.0)
        for r in range(momenta):
            re, im = real[r]
            real_scr[pair, :, lanes(0, r)] = re
            real_scr[pair, :, lanes(1, r)] = im
            mre, mim = (across(x) for x in real[-r % momenta])
            if start is not None:
                mre, mim = (jnp.where(diagonal, x, y) for x, y in zip(real[-r % momenta], (mre, mim)))
            product_scr[pair, :, lanes(0, r)] = re * mre - im * mim
            product_scr[pair, :, lanes(1, r)] = re * mim + im * mre
        return carry

    lax.fori_loop(0, all_pairs, forward, 0)
    product = product_scr[...].reshape(all_pairs * rows2, -1).astype(BF16)
    bubble = jnp.dot(weight_ref[...], product, preferred_element_type=F32)
    product_scr[...] = bubble.reshape(product_scr.shape)

    def backward(pair, carry):
        orb, local = pair // pairs, pair % pairs
        values = []
        for r in range(momenta):
            re, im = (real_scr[pair, :, lanes(part, r)] for part in range(2))
            bre, bim = (product_scr[pair, :, lanes(part, r)] * factor for part in range(2))
            values.append((re * bre - im * bim, re * bim + im * bre))
        values = dft(values, -1.0)
        for w in range(wide):
            for k in range(per_device):
                for part in range(2):
                    block_scr[w * orbs + orb, k, part, local] = values[w * per_device + k][part].astype(BF16)
        return carry

    lax.fori_loop(0, all_pairs, backward, 0)
    emit(block_scr, me, out_refs, sent_spots)


def near_kernel(*refs):
    for z, ref in enumerate(refs[:-1]):
        refs[-1][z] = ref[1]


def plane_kernel(far, *refs):
    came_ref, out_refs = refs[far], refs[far + 1 :]
    for m, out_ref in enumerate(out_refs):
        for z in range(far):
            out_ref[0, z] = refs[z][0, m]
            out_ref[1, z] = came_ref[z, m]


def langreth_kernel(came_spots, device_ref, *refs):
    left_scr, block_scr, green_scr, sems = refs[-4:]
    kinds = green_scr.shape[0]
    count, momenta, _, orbs, rows2, half = block_scr.shape[1:]
    total = kinds * orbs
    out_ref, green_any, self_refs = refs[-5], refs[-5 - total : -5], refs[: -5 - total]
    copies = [
        pltpu.make_async_copy(green_any[n], green_scr.at[n // orbs, n % orbs], sems.at[n]) for n in range(total)
    ]
    for copy in copies:
        copy.start()
    here = device_ref[0]
    me = here % orbs
    rows = rows2 // 2
    chunks = len(came_spots)
    for n, spots in enumerate(came_spots):
        used = entries(spots)
        collect(block_scr.at[n], here, self_refs[:used], spots)
        self_refs = self_refs[used:]
    row, col = grid_masks(half)
    lower, upper = row >= col, row < col
    keep = {1: lower.astype(F32).astype(BF16), -1: upper.astype(F32).astype(BF16)}
    scale = (2 * half) ** -0.5
    blocks = ((0, 0), (0, 1), (1, 0), (1, 1))
    for k in range(momenta):
        for turn in range(orbs):
            c = me ^ turn
            for part in range(2):
                sheets = {}
                for n in range(chunks):
                    piece = block_scr[n, :, k, part, c].astype(F32)
                    for index in range(2):
                        sheet = jnp.concatenate([piece[d, index * rows : (index + 1) * rows] for d in range(count)], 0)
                        for low in range(2) if chunks == 1 else (n,):
                            sheets[index, low] = sheet[low * half : (low + 1) * half] if chunks == 1 else sheet

                own, facing = sheets[0, 1], sheets[1, 1].T
                pieces = [
                    jnp.where(lower, own, 0.0),
                    sheets[1, 0].T,
                    jnp.where(lower, facing, 0.0),
                    jnp.where(upper, facing, 0.0),
                    sheets[0, 0],
                    jnp.where(upper, own, 0.0),
                ]
                at = slice(turn * half, (turn + 1) * half)
                for n, piece in enumerate(pieces):
                    left_scr[(2 * n + part) * half : (2 * n + part + 1) * half, at] = piece.astype(BF16)

        if k == 0:
            for copy in copies:
                copy.wait()
        for turn_b in range(orbs):
            b = me ^ turn_b

            def block(turn, pair, part, i, j, mask):
                kind, n = (int(i == j), i) if kinds == 2 else (0, (i == j) * 2 + i)
                piece = green_scr[kind, turn, part * orbs + pair, n, k]
                return piece * keep[mask] if mask else piece

            def left(first, last):
                return left_scr[2 * first * half : 2 * last * half, :]

            def rows_of(product, n):
                return (product[2 * n * half : (2 * n + 1) * half], product[(2 * n + 1) * half : (2 * n + 2) * half])

            def plain(first, last, i, j, mask):
                right = jnp.concatenate(
                    [
                        jnp.concatenate([block(turn, b, part, i, j, mask) for part in range(2)], 1)
                        for turn in range(orbs)
                    ],
                    0,
                )
                product = jnp.dot(left(first, last), right, preferred_element_type=F32)
                out = []
                for n in range(last - first):
                    real, imag = rows_of(product, n)
                    out.append((real[:, :half] - imag[:, half:], real[:, half:] + imag[:, :half]))
                return out

            def adjoint(first, last, i, j, mask):
                right = jnp.concatenate(
                    [
                        jnp.concatenate([block(turn_b, me ^ turn, part, i, j, mask) for part in range(2)], 0)
                        for turn in range(orbs)
                    ],
                    1,
                )
                product = lax.dot_general(
                    left(first, last), right, (((1,), (1,)), ((), ())), preferred_element_type=F32
                )
                out = []
                for n in range(last - first):
                    real, imag = rows_of(product, n)
                    out.append((real[:, :half] + imag[:, half:], imag[:, :half] - real[:, half:]))
                return out

            d1 = plain(0, 2, 0, 0, 1)
            d2 = plain(0, 2, 0, 1, 0)
            d3 = plain(0, 1, 0, 0, -1)[0]
            d4 = plain(2, 3, 1, 0, 0)[0]
            d5 = plain(2, 3, 1, 1, 1)[0]
            d6 = plain(2, 3, 1, 1, -1)[0]
            d7 = adjoint(3, 4, 0, 0, 1)[0]
            d8 = adjoint(3, 4, 1, 0, 0)[0]
            d9 = adjoint(4, 6, 1, 1, 1)
            for part in range(2):
                results = (
                    jnp.where(lower, d1[0][part], d3[part] + d7[part]),
                    d2[0][part] + d8[part] + d9[0][part],
                    d1[1][part] + d4[part],
                    jnp.where(lower, d5[part], d2[1][part] + d6[part] + d9[1][part]),
                )
                for (i, j), result in zip(blocks, results):
                    out_ref[part, k, b, i * half : (i + 1) * half, j * half : (j + 1) * half] = (
                        result * scale
                    ).astype(BF16)


def exchange(axes, count, sent):
    def shift(x, mask):
        return lax.ppermute(x, axes, [(i, i ^ mask) for i in range(count)])

    far, planes, block = len(sent), sent[0].shape[1], sent[0].shape[2:]
    far_sent = [shift(x, 2 * planes * z) if z else x for z, x in enumerate(sent)]
    swap = pl.pallas_call(
        near_kernel,
        out_shape=jax.ShapeDtypeStruct((far, planes) + block, BF16),
        in_specs=[VMEM] * far,
        out_specs=VMEM,
        compiler_params=limit(4),
        name="near",
    )(*far_sent)
    came = shift(swap, 1)
    joined = pl.pallas_call(
        functools.partial(plane_kernel, far),
        out_shape=[jax.ShapeDtypeStruct((2, far) + block, BF16)] * planes,
        in_specs=[VMEM] * (far + 1),
        out_specs=[VMEM] * planes,
        compiler_params=limit(4),
        name="plane",
    )(*far_sent, came)
    return [shift(x, 2 * m) if m else x for m, x in enumerate(joined)]


def gather(orbs, raw):
    held = {0: raw}
    bit = orbs // 2
    while bit:
        swap = [(i, i ^ bit) for i in range(orbs)]
        for turn, piece in list(held.items()):
            held[turn ^ bit] = lax.ppermute(piece, "orb", swap)
        bit //= 2
    return [held[turn] for turn in range(orbs)]


def local(wide, orbs, green, bubble_weight, tile_owner, pairing):
    parts, momenta, pairs, times, _ = green.shape
    all_pairs = bubble_weight.shape[0]
    half = times // 2
    count = wide * orbs
    chunks = 2 if half % count == 0 else 1
    rows2 = 2 * times // count // chunks
    axes = ("wide", "orb")
    planes = min(4, count // 2)
    far = count // (2 * planes)
    block = (momenta, parts, pairs, rows2, half)
    device = lax.axis_index(axes).astype(jnp.int32).reshape(1)
    spread = jnp.kron(bubble_weight, jnp.eye(rows2, dtype=F32)).astype(BF16)
    width = parts * momenta * wide * half

    off, on = ((0, 1), (1, 0)), ((0, 0), (1, 1))
    plan = [("d", on, 0, True), ("o", off, None, False)] if chunks == 2 else [("o", off + on, -half, False)]
    returned, greens, came_spots = {}, {}, {}

    def sheets(staged):
        if staged:
            return [jax.ShapeDtypeStruct((2, planes) + block, BF16)] * far
        return [jax.ShapeDtypeStruct((count,) + block, BF16)]

    def deliver(staged, sent):
        if staged:
            return exchange(axes, count, sent)
        return [lax.all_to_all(sent[0], axes, 0, 0, tiled=True)]

    for tag, blocks, start, staged in plan:
        sent_spots = places(count, 2 * planes, True) if staged else None
        came_spots[tag] = places(count, 2 * planes, False) if staged else None
        raw, *sent = pl.pallas_call(
            functools.partial(pack_kernel, blocks, sent_spots),
            out_shape=[jax.ShapeDtypeStruct((parts * pairs, len(blocks), momenta, half, half), BF16)]
            + sheets(staged),
            in_specs=[SMEM, HBM],
            out_specs=[HBM] + [VMEM] * len(sheets(staged)),
            scratch_shapes=[
                pltpu.VMEM((count,) + block, BF16),
                pltpu.VMEM((parts * pairs, len(blocks), momenta, half, half), BF16),
                pltpu.SemaphoreType.DMA((2, parts * pairs, len(blocks))),
            ],
            compiler_params=limit(8),
        )(device, green)
        greens[tag] = gather(orbs, raw)
        arrived = deliver(staged, sent)
        sent = pl.pallas_call(
            functools.partial(middle_kernel, start, came_spots[tag], sent_spots),
            out_shape=sheets(staged),
            in_specs=[SMEM] + [VMEM] * (1 + len(arrived)),
            out_specs=[VMEM] * len(sheets(staged)),
            scratch_shapes=[pltpu.VMEM((all_pairs, rows2, width), F32)] * 2 + [pltpu.VMEM((count,) + block, BF16)],
            compiler_params=limit(16),
        )(device, spread, *arrived)
        returned[tag] = deliver(staged, sent)

    tags = sorted(returned, reverse=True)
    came_spots = [came_spots[tag] for tag in tags]
    returned = sum((returned[tag] for tag in tags), [])
    raws = sum((greens[tag] for tag in tags), [])
    return pl.pallas_call(
        functools.partial(langreth_kernel, came_spots),
        out_shape=jax.ShapeDtypeStruct(green.shape, BF16),
        in_specs=[SMEM] + [VMEM] * len(returned) + [HBM] * len(raws),
        out_specs=VMEM,
        scratch_shapes=[
            pltpu.VMEM((12 * half, orbs * half), BF16),
            pltpu.VMEM((chunks, count) + block, BF16),
            pltpu.VMEM((chunks, orbs) + raws[0].shape, BF16),
            pltpu.SemaphoreType.DMA((len(raws),)),
        ],
        compiler_params=limit(60),
        name="langreth",
    )(device, *returned, *raws)


def solution(mesh):
    return jax.shard_map(
        functools.partial(local, mesh.shape["wide"], mesh.shape["orb"]),
        mesh=mesh,
        in_specs=(P(None, "wide", "orb", None, None), P(), P(), P()),
        out_specs=P(None, "wide", "orb", None, None),
        check_vma=False,
    )
```

```python
import functools
import math

import jax
import jax.numpy as jnp
from jax import lax
from jax.experimental import pallas as pl
from jax.experimental.pallas import tpu as pltpu
from jax.sharding import PartitionSpec as P


F32 = jnp.float32
BF16 = jnp.bfloat16
VMEM = pl.BlockSpec(memory_space=pltpu.VMEM)
SMEM = pl.BlockSpec(memory_space=pltpu.SMEM)
HBM = pl.BlockSpec(memory_space=pltpu.HBM)


def limit(mebibytes):
    return pltpu.CompilerParams(vmem_limit_bytes=mebibytes * 1024 * 1024)


def grid_masks(half):
    rows = lax.broadcasted_iota(jnp.int32, (half, half), 0)
    cols = lax.broadcasted_iota(jnp.int32, (half, half), 1)
    return rows, cols


def places(count, near, sent):
    if sent:
        return [(rel // near, (rel % 2, rel % near // 2)) for rel in range(count)]
    return [(rel % near // 2, (rel % 2, rel // near)) for rel in range(count)]


def emit(block_scr, me, out_refs, spots):
    if spots is None:
        out_refs[0][...] = block_scr[...]
        return
    for rel, (n, at) in enumerate(spots):
        out_refs[n].at[at][...] = block_scr[me ^ rel]


def collect(block_scr, me, in_refs, spots):
    if spots is None:
        block_scr[...] = in_refs[0][...]
        return
    for rel, (n, at) in enumerate(spots):
        block_scr[me ^ rel] = in_refs[n].at[at][...]


def entries(spots):
    return 1 if spots is None else 1 + max(n for n, _ in spots)


def halves(own, facing, count):
    rows = own.shape[0] // count
    return [
        jnp.concatenate([own[d * rows : (d + 1) * rows], facing[d * rows : (d + 1) * rows]], 0)
        for d in range(count)
    ]


def pack_kernel(blocks, spots, device_ref, green_ref, *refs):
    raw_ref, out_refs, block_scr, sems = refs[0], refs[1:-2], refs[-2], refs[-1]
    count, momenta, parts, pairs, _, half = block_scr.shape
    row, col = grid_masks(half)

    def fetch(step):
        part, pair = step // pairs, step % pairs
        return [
            pltpu.make_async_copy(
                green_ref.at[part, :, pair, pl.ds(i * half, half), pl.ds(j * half, half)],
                raw_ref.at[step, n],
                sems.at[step, n],
            )
            for n, (i, j) in enumerate(blocks)
        ]

    def begin(step, carry):
        for copy in fetch(step):
            copy.start()
        return carry

    lax.fori_loop(0, parts * pairs, begin, 0)

    def one(step, carry):
        part, pair = step // pairs, step % pairs
        for copy in fetch(step):
            copy.wait()
        for k in range(momenta):
            got = {at: raw_ref[step, n, k].astype(F32) for n, at in enumerate(blocks)}
            own, facing = [], []
            if (0, 1) in got:
                own.append(got[0, 1])
                facing.append(got[1, 0].T)
            if (0, 0) in got:
                own.append(jnp.where(row >= col, got[0, 0], got[1, 1]))
                facing.append(jnp.where(row < col, got[0, 0], got[1, 1]).T)
            own, facing = (jnp.concatenate(x, 0) if len(x) > 1 else x[0] for x in (own, facing))
            for d, piece in enumerate(halves(own, facing, count)):
                block_scr[d, k, part, pair] = piece.astype(BF16)
        return carry

    lax.fori_loop(0, parts * pairs, one, 0)
    emit(block_scr, device_ref[0], out_refs, spots)


def twiddle(re, im, angle):
    cos, sin = math.cos(angle), math.sin(angle)
    if abs(sin) < 1e-12:
        return (re, im) if cos > 0 else (-re, -im)
    if abs(cos) < 1e-12:
        return (-im, re) if sin > 0 else (im, -re)
    return re * cos - im * sin, re * sin + im * cos


def dft(values, sign):
    size = len(values)
    if size == 1:
        return values
    out = [None] * size
    if size % 2:
        for r in range(size):
            terms = [twiddle(*values[k], sign * 2 * math.pi * (k * r % size) / size) for k in range(size)]
            out[r] = (sum(t[0] for t in terms), sum(t[1] for t in terms))
        return out
    even, odd = dft(values[0::2], sign), dft(values[1::2], sign)
    for r in range(size // 2):
        re, im = twiddle(*odd[r], sign * 2 * math.pi * r / size)
        out[r] = (even[r][0] + re, even[r][1] + im)
        out[r + size // 2] = (even[r][0] - re, even[r][1] - im)
    return out


def middle_kernel(start, came_spots, sent_spots, device_ref, weight_ref, *refs):
    real_scr, product_scr, block_scr = refs[-3:]
    count, per_device, _, pairs, rows2, half = block_scr.shape
    all_pairs = weight_ref.shape[0] // rows2
    orbs = all_pairs // pairs
    wide = count // orbs
    momenta = wide * per_device
    factor = momenta ** -0.5
    me = device_ref[0]
    inputs = entries(came_spots)
    in_refs, out_refs = refs[:inputs], refs[inputs:-3]
    rows = rows2 // 2
    if start is not None:
        spot = lax.broadcasted_iota(jnp.int32, (rows2, half), 0)
        spot = jnp.where(spot >= rows, spot - rows, spot) + (me * rows + start)
        diagonal = spot == lax.broadcasted_iota(jnp.int32, (rows2, half), 1)

    collect(block_scr, me, in_refs, came_spots)

    def lanes(part, r):
        return pl.ds((part * momenta + r) * half, half)

    def across(x):
        if rows2 == 8:
            return pltpu.roll(x, rows, 0)
        return jnp.concatenate([x[rows:], x[:rows]], 0)

    def forward(pair, carry):
        orb, local = pair // pairs, pair % pairs
        values = [
            tuple(block_scr[w * orbs + orb, k, part, local].astype(F32) * factor for part in range(2))
            for w in range(wide)
            for k in range(per_device)
        ]
        real = dft(values, 1.0)
        for r in range(momenta):
            re, im = real[r]
            real_scr[pair, :, lanes(0, r)] = re
            real_scr[pair, :, lanes(1, r)] = im
            mre, mim = (across(x) for x in real[-r % momenta])
            if start is not None:
                mre, mim = (jnp.where(diagonal, x, y) for x, y in zip(real[-r % momenta], (mre, mim)))
            product_scr[pair, :, lanes(0, r)] = re * mre - im * mim
            product_scr[pair, :, lanes(1, r)] = re * mim + im * mre
        return carry

    lax.fori_loop(0, all_pairs, forward, 0)
    product = product_scr[...].reshape(all_pairs * rows2, -1).astype(BF16)
    bubble = jnp.dot(weight_ref[...], product, preferred_element_type=F32)
    product_scr[...] = bubble.reshape(product_scr.shape)

    def backward(pair, carry):
        orb, local = pair // pairs, pair % pairs
        values = []
        for r in range(momenta):
            re, im = (real_scr[pair, :, lanes(part, r)] for part in range(2))
            bre, bim = (product_scr[pair, :, lanes(part, r)] * factor for part in range(2))
            values.append((re * bre - im * bim, re * bim + im * bre))
        values = dft(values, -1.0)
        for w in range(wide):
            for k in range(per_device):
                for part in range(2):
                    block_scr[w * orbs + orb, k, part, local] = values[w * per_device + k][part].astype(BF16)
        return carry

    lax.fori_loop(0, all_pairs, backward, 0)
    emit(block_scr, me, out_refs, sent_spots)


def near_kernel(*refs):
    for z, ref in enumerate(refs[:-1]):
        refs[-1][z] = ref[1]


def plane_kernel(far, *refs):
    came_ref, out_refs = refs[far], refs[far + 1 :]
    for m, out_ref in enumerate(out_refs):
        for z in range(far):
            out_ref[0, z] = refs[z][0, m]
            out_ref[1, z] = came_ref[z, m]


SUMS = ("00", "01", "10", "r11", "l11")
SLOTS = {"o": ("10", "01"), "d": ("s00", "s11", "t00", "t11")}


def left_kernel(kinds, spots, device_ref, *refs):
    self_refs, left_ref, block_scr = refs[:-2], refs[-2], refs[-1]
    count, momenta, _, orbs, rows2, half = block_scr.shape
    rows = rows2 // 2
    here = device_ref[0]
    me = here % orbs
    collect(block_scr, here, self_refs, spots)
    row, col = grid_masks(half)
    lower, upper = row >= col, row < col
    for k in range(momenta):
        for turn in range(orbs):
            c = me ^ turn
            for part in range(2):
                sheets = {}
                piece = block_scr[:, k, part, c].astype(F32)
                for index in range(2):
                    sheet = jnp.concatenate([piece[d, index * rows : (index + 1) * rows] for d in range(count)], 0)
                    for n, kind in enumerate(kinds):
                        sheets[index, kind] = sheet[n * half : (n + 1) * half]
                pieces = []
                if "o" in kinds:
                    pieces += [sheets[1, "o"].T, sheets[0, "o"]]
                if "d" in kinds:
                    own, facing = sheets[0, "d"], sheets[1, "d"].T
                    pieces += [
                        jnp.where(lower, own, 0.0),
                        jnp.where(lower, facing, 0.0),
                        jnp.where(upper, facing, 0.0),
                        jnp.where(upper, own, 0.0),
                    ]
                at = slice(turn * half, (turn + 1) * half)
                for n, piece in enumerate(pieces):
                    left_ref[k, (2 * n + part) * half : (2 * n + part + 1) * half, at] = piece.astype(BF16)


def langreth_kernel(kinds, sums_in, sums_out, device_ref, left_ref, *refs):
    if sums_in:
        sums_ref, green_scr, out_ref = refs
    else:
        out_ref, green_scr, sems = refs[-3:]
    held, orbs = green_scr.shape[:2]
    momenta, half = green_scr.shape[-3:-1]
    copies = []
    if not sums_in:
        copies = [
            pltpu.make_async_copy(green_any, green_scr.at[n // orbs, n % orbs], sems.at[n])
            for n, green_any in enumerate(refs[:-3])
        ]
    for copy in copies:
        copy.start()
    me = device_ref[0] % orbs
    row, col = grid_masks(half)
    lower, upper = row >= col, row < col
    keep = {1: lower.astype(F32).astype(BF16), -1: upper.astype(F32).astype(BF16)}
    scale = (2 * half) ** -0.5
    blocks = ((0, 0), (0, 1), (1, 0), (1, 1))
    slots = sum((SLOTS[kind] for kind in kinds), ())
    for k in range(momenta):
        if k == 0:
            for copy in copies:
                copy.wait()
        for turn_b in range(orbs):
            b = me ^ turn_b

            def block(turn, pair, part, i, j, mask):
                kind, n = (int(i == j), i) if held == 2 else (0, (i == j) * 2 + i)
                piece = green_scr[kind, turn, part * orbs + pair, n, k]
                return piece * keep[mask] if mask else piece

            def left(slot):
                n = slots.index(slot)
                return left_ref[k, 2 * n * half : 2 * (n + 1) * half, :]

            def plain(slot, i, j, mask):
                right = jnp.concatenate(
                    [
                        jnp.concatenate([block(turn, b, part, i, j, mask) for part in range(2)], 1)
                        for turn in range(orbs)
                    ],
                    0,
                )
                product = jnp.dot(left(slot), right, preferred_element_type=F32)
                real, imag = product[:half], product[half:]
                return real[:, :half] - imag[:, half:], real[:, half:] + imag[:, :half]

            def adjoint(slot, i, j, mask):
                right = jnp.concatenate(
                    [
                        jnp.concatenate([block(turn_b, me ^ turn, part, i, j, mask) for part in range(2)], 0)
                        for turn in range(orbs)
                    ],
                    1,
                )
                product = lax.dot_general(
                    left(slot), right, (((1,), (1,)), ((), ())), preferred_element_type=F32
                )
                real, imag = product[:half], product[half:]
                return real[:, :half] + imag[:, half:], imag[:, :half] - real[:, half:]

            def total_of(*terms):
                return tuple(sum(term[part] for term in terms) for part in range(2))

            terms = {name: [] for name in SUMS}
            if sums_in:
                for n, name in enumerate(SUMS):
                    terms[name].append(tuple(sums_ref[n, part, k, b] for part in range(2)))
            if "o" in kinds:
                terms["01"].append(adjoint("01", 1, 1, 1))
                terms["10"].append(plain("10", 0, 0, 1))
                terms["l11"].append(plain("10", 0, 1, 0))
            if "d" in kinds:
                retarded = plain("s00", 0, 0, 1)
                lesser = total_of(plain("s00", 0, 0, -1), adjoint("t00", 0, 0, 1))
                terms["00"].append(tuple(jnp.where(lower, r, l) for r, l in zip(retarded, lesser)))
                terms["01"] += [plain("s00", 0, 1, 0), adjoint("t00", 1, 0, 0)]
                terms["10"].append(plain("s11", 1, 0, 0))
                terms["r11"].append(plain("s11", 1, 1, 1))
                terms["l11"] += [plain("s11", 1, 1, -1), adjoint("t11", 1, 1, 1)]
            got = {name: total_of(*terms[name]) for name in SUMS}
            if sums_out:
                for n, name in enumerate(SUMS):
                    for part in range(2):
                        out_ref[n, part, k, b] = got[name][part]
                continue
            for part in range(2):
                results = (
                    got["00"][part],
                    got["01"][part],
                    got["10"][part],
                    jnp.where(lower, got["r11"][part], got["l11"][part]),
                )
                for (i, j), result in zip(blocks, results):
                    out_ref[part, k, b, i * half : (i + 1) * half, j * half : (j + 1) * half] = (
                        result * scale
                    ).astype(BF16)


def exchange(axes, count, sent):
    def shift(x, mask):
        return lax.ppermute(x, axes, [(i, i ^ mask) for i in range(count)])

    far, planes, block = len(sent), sent[0].shape[1], sent[0].shape[2:]
    far_sent = [shift(x, 2 * planes * z) if z else x for z, x in enumerate(sent)]
    swap = pl.pallas_call(
        near_kernel,
        out_shape=jax.ShapeDtypeStruct((far, planes) + block, BF16),
        in_specs=[VMEM] * far,
        out_specs=VMEM,
        compiler_params=limit(4),
        name="near",
    )(*far_sent)
    came = shift(swap, 1)
    joined = pl.pallas_call(
        functools.partial(plane_kernel, far),
        out_shape=[jax.ShapeDtypeStruct((2, far) + block, BF16)] * planes,
        in_specs=[VMEM] * (far + 1),
        out_specs=[VMEM] * planes,
        compiler_params=limit(4),
        name="plane",
    )(*far_sent, came)
    return [shift(x, 2 * m) if m else x for m, x in enumerate(joined)]


def gather(orbs, raw):
    held = {0: raw}
    bit = orbs // 2
    while bit:
        swap = [(i, i ^ bit) for i in range(orbs)]
        for turn, piece in list(held.items()):
            held[turn ^ bit] = lax.ppermute(piece, "orb", swap)
        bit //= 2
    return [held[turn] for turn in range(orbs)]


def local(wide, orbs, green, bubble_weight, tile_owner, pairing):
    parts, momenta, pairs, times, _ = green.shape
    all_pairs = bubble_weight.shape[0]
    half = times // 2
    count = wide * orbs
    chunks = 2 if half % count == 0 else 1
    rows2 = 2 * times // count // chunks
    axes = ("wide", "orb")
    planes = min(4, count // 2)
    far = count // (2 * planes)
    block = (momenta, parts, pairs, rows2, half)
    device = lax.axis_index(axes).astype(jnp.int32).reshape(1)
    spread = jnp.kron(bubble_weight, jnp.eye(rows2, dtype=F32)).astype(BF16)
    width = parts * momenta * wide * half

    off, on = ((0, 1), (1, 0)), ((0, 0), (1, 1))
    if chunks == 2:
        plan = [("d", on, 0, True, False), ("o", off, None, False, True)]
    else:
        plan = [("o", off + on, -half, False, False)]
    returned, greens, came_spots = {}, {}, {}

    def sheets(staged):
        if staged:
            return [jax.ShapeDtypeStruct((2, planes) + block, BF16)] * far
        return [jax.ShapeDtypeStruct((count,) + block, BF16)]

    def deliver(staged, sent):
        if staged:
            return exchange(axes, count, sent)
        return [lax.all_to_all(sent[0], axes, 0, 0, tiled=True)]

    def spots(staged, sent):
        return places(count, 2 * planes, sent) if staged else None

    for tag, blocks, start, staged, staged_back in plan:
        came_spots[tag] = spots(staged_back, False)
        raw, *sent = pl.pallas_call(
            functools.partial(pack_kernel, blocks, spots(staged, True)),
            out_shape=[jax.ShapeDtypeStruct((parts * pairs, len(blocks), momenta, half, half), BF16)]
            + sheets(staged),
            in_specs=[SMEM, HBM],
            out_specs=[VMEM] * (1 + len(sheets(staged))),
            scratch_shapes=[pltpu.VMEM((count,) + block, BF16), pltpu.SemaphoreType.DMA((parts * pairs, len(blocks)))],
            compiler_params=limit(8),
        )(device, green)
        greens[tag] = gather(orbs, raw)
        arrived = deliver(staged, sent)
        sent = pl.pallas_call(
            functools.partial(middle_kernel, start, spots(staged, False), spots(staged_back, True)),
            out_shape=sheets(staged_back),
            in_specs=[SMEM] + [VMEM] * (1 + len(arrived)),
            out_specs=[VMEM] * len(sheets(staged_back)),
            scratch_shapes=[pltpu.VMEM((all_pairs, rows2, width), F32)] * 2 + [pltpu.VMEM((count,) + block, BF16)],
            compiler_params=limit(16),
        )(device, spread, *arrived)
        returned[tag] = deliver(staged_back, sent)

    raws = sum((greens[tag] for tag in sorted(greens, reverse=True)), [])
    sums_shape = jax.ShapeDtypeStruct((len(SUMS), parts, momenta, pairs, half, half), F32)
    final = jax.ShapeDtypeStruct(green.shape, BF16)

    held = jax.ShapeDtypeStruct((chunks, orbs) + raws[0].shape, BF16)

    def left(kinds, tag):
        slots = sum(len(SLOTS[kind]) for kind in kinds)
        return pl.pallas_call(
            functools.partial(left_kernel, kinds, came_spots[tag]),
            out_shape=jax.ShapeDtypeStruct((momenta, 2 * slots * half, orbs * half), BF16),
            in_specs=[SMEM] + [VMEM] * len(returned[tag]),
            out_specs=VMEM,
            scratch_shapes=[pltpu.VMEM((count,) + block, BF16)],
            compiler_params=limit(16),
        )(device, *returned[tag])

    def langreth(kinds, tag, sums, out_shape):
        return pl.pallas_call(
            functools.partial(langreth_kernel, kinds, len(sums) > 0, out_shape is sums_shape),
            out_shape=out_shape if sums else [out_shape, held],
            in_specs=[SMEM] + [VMEM] * (1 + len(sums)) + [HBM] * (0 if sums else len(raws)),
            out_specs=VMEM if sums else [VMEM, VMEM],
            scratch_shapes=[] if sums else [pltpu.SemaphoreType.DMA((len(raws),))],
            compiler_params=limit(20),
            name="langreth",
        )(device, left(kinds, tag), *sums, *([] if sums else raws))

    if chunks == 1:
        return langreth(("o", "d"), "o", [], final)[0]
    sums = langreth(("d",), "d", [], sums_shape)
    return langreth(("o",), "o", sums, final)


def solution(mesh):
    return jax.shard_map(
        functools.partial(local, mesh.shape["wide"], mesh.shape["orb"]),
        mesh=mesh,
        in_specs=(P(None, "wide", "orb", None, None), P(), P(), P()),
        out_specs=P(None, "wide", "orb", None, None),
        check_vma=False,
    )
```

```python
import functools
import math

import jax
import jax.numpy as jnp
from jax import lax
from jax.experimental import pallas as pl
from jax.experimental.pallas import tpu as pltpu
from jax.sharding import PartitionSpec as P


F32 = jnp.float32
BF16 = jnp.bfloat16
VMEM = pl.BlockSpec(memory_space=pltpu.VMEM)
SMEM = pl.BlockSpec(memory_space=pltpu.SMEM)
HBM = pl.BlockSpec(memory_space=pltpu.HBM)


def limit(mebibytes):
    return pltpu.CompilerParams(vmem_limit_bytes=mebibytes * 1024 * 1024)


def grid_masks(half):
    rows = lax.broadcasted_iota(jnp.int32, (half, half), 0)
    cols = lax.broadcasted_iota(jnp.int32, (half, half), 1)
    return rows, cols


def places(count, near, sent):
    if sent:
        return [(rel // near, (rel % 2, rel % near // 2)) for rel in range(count)]
    return [(rel % near // 2, (rel % 2, rel // near)) for rel in range(count)]


def emit(block_scr, me, out_refs, spots):
    if spots is None:
        out_refs[0][...] = block_scr[...]
        return
    for rel, (n, at) in enumerate(spots):
        out_refs[n].at[at][...] = block_scr[me ^ rel]


def collect(block_scr, me, in_refs, spots):
    if spots is None:
        block_scr[...] = in_refs[0][...]
        return
    for rel, (n, at) in enumerate(spots):
        block_scr[me ^ rel] = in_refs[n].at[at][...]


def entries(spots):
    return 1 if spots is None else 1 + max(n for n, _ in spots)


def halves(own, facing, count):
    rows = own.shape[0] // count
    return [
        jnp.concatenate([own[d * rows : (d + 1) * rows], facing[d * rows : (d + 1) * rows]], 0)
        for d in range(count)
    ]


def pack_kernel(blocks, spots, device_ref, green_ref, *refs):
    raw_ref, out_refs, block_scr = refs[0], refs[1:-1], refs[-1]
    count, momenta, parts, pairs, _, half = block_scr.shape
    row, col = grid_masks(half)

    def one(step, carry):
        part, pair = step // pairs, step % pairs
        for k in range(momenta):
            got = {}
            for n, (i, j) in enumerate(blocks):
                piece = green_ref[part, k, pair, i * half : (i + 1) * half, j * half : (j + 1) * half]
                raw_ref[step, n, k] = piece
                got[i, j] = piece.astype(F32)
            own, facing = [], []
            if (0, 1) in got:
                own.append(got[0, 1])
                facing.append(got[1, 0].T)
            if (0, 0) in got:
                own.append(jnp.where(row >= col, got[0, 0], got[1, 1]))
                facing.append(jnp.where(row < col, got[0, 0], got[1, 1]).T)
            own, facing = (jnp.concatenate(x, 0) if len(x) > 1 else x[0] for x in (own, facing))
            for d, piece in enumerate(halves(own, facing, count)):
                block_scr[d, k, part, pair] = piece.astype(BF16)
        return carry

    lax.fori_loop(0, parts * pairs, one, 0)
    emit(block_scr, device_ref[0], out_refs, spots)


def twiddle(re, im, angle):
    cos, sin = math.cos(angle), math.sin(angle)
    if abs(sin) < 1e-12:
        return (re, im) if cos > 0 else (-re, -im)
    if abs(cos) < 1e-12:
        return (-im, re) if sin > 0 else (im, -re)
    return re * cos - im * sin, re * sin + im * cos


def dft(values, sign):
    size = len(values)
    if size == 1:
        return values
    out = [None] * size
    if size % 2:
        for r in range(size):
            terms = [twiddle(*values[k], sign * 2 * math.pi * (k * r % size) / size) for k in range(size)]
            out[r] = (sum(t[0] for t in terms), sum(t[1] for t in terms))
        return out
    even, odd = dft(values[0::2], sign), dft(values[1::2], sign)
    for r in range(size // 2):
        re, im = twiddle(*odd[r], sign * 2 * math.pi * r / size)
        out[r] = (even[r][0] + re, even[r][1] + im)
        out[r + size // 2] = (even[r][0] - re, even[r][1] - im)
    return out


def middle_kernel(start, came_spots, sent_spots, device_ref, weight_ref, *refs):
    real_scr, product_scr, block_scr = refs[-3:]
    count, per_device, _, pairs, rows2, half = block_scr.shape
    all_pairs = weight_ref.shape[0] // rows2
    orbs = all_pairs // pairs
    wide = count // orbs
    momenta = wide * per_device
    factor = momenta ** -0.5
    me = device_ref[0]
    inputs = entries(came_spots)
    in_refs, out_refs = refs[:inputs], refs[inputs:-3]
    rows = rows2 // 2
    if start is not None:
        spot = lax.broadcasted_iota(jnp.int32, (rows2, half), 0)
        spot = jnp.where(spot >= rows, spot - rows, spot) + (me * rows + start)
        diagonal = spot == lax.broadcasted_iota(jnp.int32, (rows2, half), 1)

    collect(block_scr, me, in_refs, came_spots)

    def lanes(part, r):
        return pl.ds((part * momenta + r) * half, half)

    def across(x):
        if rows2 == 8:
            return pltpu.roll(x, rows, 0)
        return jnp.concatenate([x[rows:], x[:rows]], 0)

    def forward(pair, carry):
        orb, local = pair // pairs, pair % pairs
        values = [
            tuple(block_scr[w * orbs + orb, k, part, local].astype(F32) * factor for part in range(2))
            for w in range(wide)
            for k in range(per_device)
        ]
        real = dft(values, 1.0)
        for r in range(momenta):
            re, im = real[r]
            real_scr[pair, :, lanes(0, r)] = re
            real_scr[pair, :, lanes(1, r)] = im
            mre, mim = (across(x) for x in real[-r % momenta])
            if start is not None:
                mre, mim = (jnp.where(diagonal, x, y) for x, y in zip(real[-r % momenta], (mre, mim)))
            product_scr[pair, :, lanes(0, r)] = re * mre - im * mim
            product_scr[pair, :, lanes(1, r)] = re * mim + im * mre
        return carry

    lax.fori_loop(0, all_pairs, forward, 0)
    product = product_scr[...].reshape(all_pairs * rows2, -1).astype(BF16)
    bubble = jnp.dot(weight_ref[...], product, preferred_element_type=F32)
    product_scr[...] = bubble.reshape(product_scr.shape)

    def backward(pair, carry):
        orb, local = pair // pairs, pair % pairs
        values = []
        for r in range(momenta):
            re, im = (real_scr[pair, :, lanes(part, r)] for part in range(2))
            bre, bim = (product_scr[pair, :, lanes(part, r)] * factor for part in range(2))
            values.append((re * bre - im * bim, re * bim + im * bre))
        values = dft(values, -1.0)
        for w in range(wide):
            for k in range(per_device):
                for part in range(2):
                    block_scr[w * orbs + orb, k, part, local] = values[w * per_device + k][part].astype(BF16)
        return carry

    lax.fori_loop(0, all_pairs, backward, 0)
    emit(block_scr, me, out_refs, sent_spots)


def near_kernel(*refs):
    for z, ref in enumerate(refs[:-1]):
        refs[-1][z] = ref[1]


def plane_kernel(far, *refs):
    came_ref, out_refs = refs[far], refs[far + 1 :]
    for m, out_ref in enumerate(out_refs):
        for z in range(far):
            out_ref[0, z] = refs[z][0, m]
            out_ref[1, z] = came_ref[z, m]


SUMS = ("00", "01", "10", "r11", "l11")
SLOTS = {"o": ("10", "01"), "d": ("s00", "s11", "t00", "t11")}


def left_kernel(kinds, spots, device_ref, *refs):
    self_refs, left_ref, block_scr = refs[:-2], refs[-2], refs[-1]
    count, momenta, _, orbs, rows2, half = block_scr.shape
    rows = rows2 // 2
    here = device_ref[0]
    me = here % orbs
    collect(block_scr, here, self_refs, spots)
    row, col = grid_masks(half)
    lower, upper = row >= col, row < col
    for k in range(momenta):
        for turn in range(orbs):
            c = me ^ turn
            for part in range(2):
                sheets = {}
                piece = block_scr[:, k, part, c].astype(F32)
                for index in range(2):
                    sheet = jnp.concatenate([piece[d, index * rows : (index + 1) * rows] for d in range(count)], 0)
                    for n, kind in enumerate(kinds):
                        sheets[index, kind] = sheet[n * half : (n + 1) * half]
                pieces = []
                if "o" in kinds:
                    pieces += [sheets[1, "o"].T, sheets[0, "o"]]
                if "d" in kinds:
                    own, facing = sheets[0, "d"], sheets[1, "d"].T
                    pieces += [
                        jnp.where(lower, own, 0.0),
                        jnp.where(lower, facing, 0.0),
                        jnp.where(upper, facing, 0.0),
                        jnp.where(upper, own, 0.0),
                    ]
                at = slice(turn * half, (turn + 1) * half)
                for n, piece in enumerate(pieces):
                    left_ref[k, (2 * n + part) * half : (2 * n + part + 1) * half, at] = piece.astype(BF16)


def langreth_kernel(kinds, sums_in, sums_out, device_ref, left_ref, *refs):
    if sums_in:
        sums_ref, green_scr, out_ref = refs
    else:
        out_ref, green_scr, sems = refs[-3:]
    held, orbs = green_scr.shape[:2]
    momenta, half = green_scr.shape[-3:-1]
    copies = []
    if not sums_in:
        copies = [
            pltpu.make_async_copy(green_any, green_scr.at[n // orbs, n % orbs], sems.at[n])
            for n, green_any in enumerate(refs[:-3])
        ]
    for copy in copies:
        copy.start()
    me = device_ref[0] % orbs
    row, col = grid_masks(half)
    lower, upper = row >= col, row < col
    keep = {1: lower.astype(F32).astype(BF16), -1: upper.astype(F32).astype(BF16)}
    scale = (2 * half) ** -0.5
    blocks = ((0, 0), (0, 1), (1, 0), (1, 1))
    slots = sum((SLOTS[kind] for kind in kinds), ())
    for k in range(momenta):
        if k == 0:
            for copy in copies:
                copy.wait()
        for turn_b in range(orbs):
            b = me ^ turn_b

            def block(turn, pair, part, i, j, mask):
                kind, n = (int(i == j), i) if held == 2 else (0, (i == j) * 2 + i)
                piece = green_scr[kind, turn, part * orbs + pair, n, k]
                return piece * keep[mask] if mask else piece

            def left(slot):
                n = slots.index(slot)
                return left_ref[k, 2 * n * half : 2 * (n + 1) * half, :]

            def plain(slot, i, j, mask):
                right = jnp.concatenate(
                    [
                        jnp.concatenate([block(turn, b, part, i, j, mask) for part in range(2)], 1)
                        for turn in range(orbs)
                    ],
                    0,
                )
                product = jnp.dot(left(slot), right, preferred_element_type=F32)
                real, imag = product[:half], product[half:]
                return real[:, :half] - imag[:, half:], real[:, half:] + imag[:, :half]

            def adjoint(slot, i, j, mask):
                right = jnp.concatenate(
                    [
                        jnp.concatenate([block(turn_b, me ^ turn, part, i, j, mask) for part in range(2)], 0)
                        for turn in range(orbs)
                    ],
                    1,
                )
                product = lax.dot_general(
                    left(slot), right, (((1,), (1,)), ((), ())), preferred_element_type=F32
                )
                real, imag = product[:half], product[half:]
                return real[:, :half] + imag[:, half:], imag[:, :half] - real[:, half:]

            def total_of(*terms):
                return tuple(sum(term[part] for term in terms) for part in range(2))

            terms = {name: [] for name in SUMS}
            if sums_in:
                for n, name in enumerate(SUMS):
                    terms[name].append(tuple(sums_ref[n, part, k, b] for part in range(2)))
            if "o" in kinds:
                terms["01"].append(adjoint("01", 1, 1, 1))
                terms["10"].append(plain("10", 0, 0, 1))
                terms["l11"].append(plain("10", 0, 1, 0))
            if "d" in kinds:
                retarded = plain("s00", 0, 0, 1)
                lesser = total_of(plain("s00", 0, 0, -1), adjoint("t00", 0, 0, 1))
                terms["00"].append(tuple(jnp.where(lower, r, l) for r, l in zip(retarded, lesser)))
                terms["01"] += [plain("s00", 0, 1, 0), adjoint("t00", 1, 0, 0)]
                terms["10"].append(plain("s11", 1, 0, 0))
                terms["r11"].append(plain("s11", 1, 1, 1))
                terms["l11"] += [plain("s11", 1, 1, -1), adjoint("t11", 1, 1, 1)]
            got = {name: total_of(*terms[name]) for name in SUMS}
            if sums_out:
                for n, name in enumerate(SUMS):
                    for part in range(2):
                        out_ref[n, part, k, b] = got[name][part]
                continue
            for part in range(2):
                results = (
                    got["00"][part],
                    got["01"][part],
                    got["10"][part],
                    jnp.where(lower, got["r11"][part], got["l11"][part]),
                )
                for (i, j), result in zip(blocks, results):
                    out_ref[part, k, b, i * half : (i + 1) * half, j * half : (j + 1) * half] = (
                        result * scale
                    ).astype(BF16)


def exchange(axes, count, sent):
    def shift(x, mask):
        return lax.ppermute(x, axes, [(i, i ^ mask) for i in range(count)])

    far, planes, block = len(sent), sent[0].shape[1], sent[0].shape[2:]
    far_sent = [shift(x, 2 * planes * z) if z else x for z, x in enumerate(sent)]
    swap = pl.pallas_call(
        near_kernel,
        out_shape=jax.ShapeDtypeStruct((far, planes) + block, BF16),
        in_specs=[VMEM] * far,
        out_specs=VMEM,
        compiler_params=limit(4),
        name="near",
    )(*far_sent)
    came = shift(swap, 1)
    joined = pl.pallas_call(
        functools.partial(plane_kernel, far),
        out_shape=[jax.ShapeDtypeStruct((2, far) + block, BF16)] * planes,
        in_specs=[VMEM] * (far + 1),
        out_specs=[VMEM] * planes,
        compiler_params=limit(4),
        name="plane",
    )(*far_sent, came)
    return [shift(x, 2 * m) if m else x for m, x in enumerate(joined)]


def gather(orbs, raw):
    held = {0: raw}
    bit = orbs // 2
    while bit:
        swap = [(i, i ^ bit) for i in range(orbs)]
        for turn, piece in list(held.items()):
            held[turn ^ bit] = lax.ppermute(piece, "orb", swap)
        bit //= 2
    return [held[turn] for turn in range(orbs)]


def local(wide, orbs, green, bubble_weight, tile_owner, pairing):
    parts, momenta, pairs, times, _ = green.shape
    all_pairs = bubble_weight.shape[0]
    half = times // 2
    count = wide * orbs
    chunks = 2 if half % count == 0 else 1
    rows2 = 2 * times // count // chunks
    axes = ("wide", "orb")
    planes = min(4, count // 2)
    far = count // (2 * planes)
    block = (momenta, parts, pairs, rows2, half)
    device = lax.axis_index(axes).astype(jnp.int32).reshape(1)
    spread = jnp.kron(bubble_weight, jnp.eye(rows2, dtype=F32)).astype(BF16)
    width = parts * momenta * wide * half

    off, on = ((0, 1), (1, 0)), ((0, 0), (1, 1))
    if chunks == 2:
        plan = [("d", on, 0, True, False), ("o", off, None, False, True)]
    else:
        plan = [("o", off + on, -half, False, False)]
    returned, greens, came_spots = {}, {}, {}

    def sheets(staged):
        if staged:
            return [jax.ShapeDtypeStruct((2, planes) + block, BF16)] * far
        return [jax.ShapeDtypeStruct((count,) + block, BF16)]

    def deliver(staged, sent):
        if staged:
            return exchange(axes, count, sent)
        return [lax.all_to_all(sent[0], axes, 0, 0, tiled=True)]

    def spots(staged, sent):
        return places(count, 2 * planes, sent) if staged else None

    for tag, blocks, start, staged, staged_back in plan:
        came_spots[tag] = spots(staged_back, False)
        raw, *sent = pl.pallas_call(
            functools.partial(pack_kernel, blocks, spots(staged, True)),
            out_shape=[jax.ShapeDtypeStruct((parts * pairs, len(blocks), momenta, half, half), BF16)]
            + sheets(staged),
            in_specs=[SMEM, VMEM],
            out_specs=[VMEM] * (1 + len(sheets(staged))),
            scratch_shapes=[pltpu.VMEM((count,) + block, BF16)],
            compiler_params=limit(8),
        )(device, green)
        greens[tag] = gather(orbs, raw)
        arrived = deliver(staged, sent)
        sent = pl.pallas_call(
            functools.partial(middle_kernel, start, spots(staged, False), spots(staged_back, True)),
            out_shape=sheets(staged_back),
            in_specs=[SMEM] + [VMEM] * (1 + len(arrived)),
            out_specs=[VMEM] * len(sheets(staged_back)),
            scratch_shapes=[pltpu.VMEM((all_pairs, rows2, width), F32)] * 2 + [pltpu.VMEM((count,) + block, BF16)],
            compiler_params=limit(16),
        )(device, spread, *arrived)
        returned[tag] = deliver(staged_back, sent)

    raws = sum((greens[tag] for tag in sorted(greens, reverse=True)), [])
    sums_shape = jax.ShapeDtypeStruct((len(SUMS), parts, momenta, pairs, half, half), F32)
    final = jax.ShapeDtypeStruct(green.shape, BF16)

    held = jax.ShapeDtypeStruct((chunks, orbs) + raws[0].shape, BF16)

    def left(kinds, tag):
        slots = sum(len(SLOTS[kind]) for kind in kinds)
        return pl.pallas_call(
            functools.partial(left_kernel, kinds, came_spots[tag]),
            out_shape=jax.ShapeDtypeStruct((momenta, 2 * slots * half, orbs * half), BF16),
            in_specs=[SMEM] + [VMEM] * len(returned[tag]),
            out_specs=VMEM,
            scratch_shapes=[pltpu.VMEM((count,) + block, BF16)],
            compiler_params=limit(16),
        )(device, *returned[tag])

    def langreth(kinds, tag, sums, out_shape):
        return pl.pallas_call(
            functools.partial(langreth_kernel, kinds, len(sums) > 0, out_shape is sums_shape),
            out_shape=out_shape if sums else [out_shape, held],
            in_specs=[SMEM] + [VMEM] * (1 + len(sums)) + [HBM] * (0 if sums else len(raws)),
            out_specs=VMEM if sums else [VMEM, VMEM],
            scratch_shapes=[] if sums else [pltpu.SemaphoreType.DMA((len(raws),))],
            compiler_params=limit(20),
            name="langreth",
        )(device, left(kinds, tag), *sums, *([] if sums else raws))

    if chunks == 1:
        return langreth(("o", "d"), "o", [], final)[0]
    sums = langreth(("d",), "d", [], sums_shape)
    return langreth(("o",), "o", sums, final)


def solution(mesh):
    return jax.shard_map(
        functools.partial(local, mesh.shape["wide"], mesh.shape["orb"]),
        mesh=mesh,
        in_specs=(P(None, "wide", "orb", None, None), P(), P(), P()),
        out_specs=P(None, "wide", "orb", None, None),
        check_vma=False,
    )
```

```python
import functools
import math

import jax
import jax.numpy as jnp
from jax import lax
from jax.experimental import pallas as pl
from jax.experimental.pallas import tpu as pltpu
from jax.sharding import PartitionSpec as P


F32 = jnp.float32
BF16 = jnp.bfloat16
VMEM = pl.BlockSpec(memory_space=pltpu.VMEM)
SMEM = pl.BlockSpec(memory_space=pltpu.SMEM)
HBM = pl.BlockSpec(memory_space=pltpu.HBM)


def limit(mebibytes):
    return pltpu.CompilerParams(vmem_limit_bytes=mebibytes * 1024 * 1024)


def grid_masks(half):
    rows = lax.broadcasted_iota(jnp.int32, (half, half), 0)
    cols = lax.broadcasted_iota(jnp.int32, (half, half), 1)
    return rows, cols


def places(count, near, sent):
    if sent:
        return [(rel // near, (rel % 2, rel % near // 2)) for rel in range(count)]
    return [(rel % near // 2, (rel % 2, rel // near)) for rel in range(count)]


def emit(block_scr, me, out_refs, spots):
    if spots is None:
        out_refs[0][...] = block_scr[...]
        return
    for rel, (n, at) in enumerate(spots):
        out_refs[n].at[at][...] = block_scr[me ^ rel]


def collect(block_scr, me, in_refs, spots):
    if spots is None:
        block_scr[...] = in_refs[0][...]
        return
    for rel, (n, at) in enumerate(spots):
        block_scr[me ^ rel] = in_refs[n].at[at][...]


def entries(spots):
    return 1 if spots is None else 1 + max(n for n, _ in spots)


def grouped(size, step, group):
    group = math.gcd(size, group)

    def several(n, carry):
        for i in range(group):
            carry = step(group * n + i, carry)
        return carry

    lax.fori_loop(0, size // group, several, 0)


def halves(own, facing, count):
    rows = own.shape[0] // count
    return [
        jnp.concatenate([own[d * rows : (d + 1) * rows], facing[d * rows : (d + 1) * rows]], 0)
        for d in range(count)
    ]


def pack_kernel(blocks, spots, device_ref, green_ref, *refs):
    raw_ref, out_refs, block_scr = refs[0], refs[1:-1], refs[-1]
    count, momenta, parts, pairs, _, half = block_scr.shape
    row, col = grid_masks(half)

    def one(step, carry):
        part, pair = step // pairs, step % pairs
        for k in range(momenta):
            got = {}
            for n, (i, j) in enumerate(blocks):
                piece = green_ref[part, k, pair, i * half : (i + 1) * half, j * half : (j + 1) * half]
                raw_ref[step, n, k] = piece
                got[i, j] = piece.astype(F32)
            own, facing = [], []
            if (0, 1) in got:
                own.append(got[0, 1])
                facing.append(got[1, 0].T)
            if (0, 0) in got:
                own.append(jnp.where(row >= col, got[0, 0], got[1, 1]))
                facing.append(jnp.where(row < col, got[0, 0], got[1, 1]).T)
            own, facing = (jnp.concatenate(x, 0) if len(x) > 1 else x[0] for x in (own, facing))
            for d, piece in enumerate(halves(own, facing, count)):
                block_scr[d, k, part, pair] = piece.astype(BF16)
        return carry

    grouped(parts * pairs, one, 8)
    emit(block_scr, device_ref[0], out_refs, spots)


def twiddle(re, im, angle):
    cos, sin = math.cos(angle), math.sin(angle)
    if abs(sin) < 1e-12:
        return (re, im) if cos > 0 else (-re, -im)
    if abs(cos) < 1e-12:
        return (-im, re) if sin > 0 else (im, -re)
    return re * cos - im * sin, re * sin + im * cos


def dft(values, sign):
    size = len(values)
    if size == 1:
        return values
    out = [None] * size
    if size % 2:
        for r in range(size):
            terms = [twiddle(*values[k], sign * 2 * math.pi * (k * r % size) / size) for k in range(size)]
            out[r] = (sum(t[0] for t in terms), sum(t[1] for t in terms))
        return out
    even, odd = dft(values[0::2], sign), dft(values[1::2], sign)
    for r in range(size // 2):
        re, im = twiddle(*odd[r], sign * 2 * math.pi * r / size)
        out[r] = (even[r][0] + re, even[r][1] + im)
        out[r + size // 2] = (even[r][0] - re, even[r][1] - im)
    return out


def middle_kernel(start, came_spots, sent_spots, device_ref, weight_ref, *refs):
    real_scr, product_scr, block_scr = refs[-3:]
    count, per_device, _, pairs, rows2, half = block_scr.shape
    all_pairs = weight_ref.shape[0] // rows2
    orbs = all_pairs // pairs
    wide = count // orbs
    momenta = wide * per_device
    factor = momenta ** -0.5
    me = device_ref[0]
    inputs = entries(came_spots)
    in_refs, out_refs = refs[:inputs], refs[inputs:-3]
    rows = rows2 // 2
    if start is not None:
        spot = lax.broadcasted_iota(jnp.int32, (rows2, half), 0)
        spot = jnp.where(spot >= rows, spot - rows, spot) + (me * rows + start)
        diagonal = spot == lax.broadcasted_iota(jnp.int32, (rows2, half), 1)

    collect(block_scr, me, in_refs, came_spots)

    def lanes(part, r):
        return pl.ds((part * momenta + r) * half, half)

    def across(x):
        if rows2 == 8:
            return pltpu.roll(x, rows, 0)
        return jnp.concatenate([x[rows:], x[:rows]], 0)

    def forward(pair, carry):
        orb, local = pair // pairs, pair % pairs
        values = [
            tuple(block_scr[w * orbs + orb, k, part, local].astype(F32) * factor for part in range(2))
            for w in range(wide)
            for k in range(per_device)
        ]
        real = dft(values, 1.0)
        for r in range(momenta):
            re, im = real[r]
            real_scr[pair, :, lanes(0, r)] = re
            real_scr[pair, :, lanes(1, r)] = im
            mre, mim = (across(x) for x in real[-r % momenta])
            if start is not None:
                mre, mim = (jnp.where(diagonal, x, y) for x, y in zip(real[-r % momenta], (mre, mim)))
            product_scr[pair, :, lanes(0, r)] = re * mre - im * mim
            product_scr[pair, :, lanes(1, r)] = re * mim + im * mre
        return carry

    grouped(all_pairs, forward, 2)
    product = product_scr[...].reshape(all_pairs * rows2, -1).astype(BF16)
    bubble = jnp.dot(weight_ref[...], product, preferred_element_type=F32)
    product_scr[...] = bubble.reshape(product_scr.shape)

    def backward(pair, carry):
        orb, local = pair // pairs, pair % pairs
        values = []
        for r in range(momenta):
            re, im = (real_scr[pair, :, lanes(part, r)] for part in range(2))
            bre, bim = (product_scr[pair, :, lanes(part, r)] * factor for part in range(2))
            values.append((re * bre - im * bim, re * bim + im * bre))
        values = dft(values, -1.0)
        for w in range(wide):
            for k in range(per_device):
                for part in range(2):
                    block_scr[w * orbs + orb, k, part, local] = values[w * per_device + k][part].astype(BF16)
        return carry

    grouped(all_pairs, backward, 2)
    emit(block_scr, me, out_refs, sent_spots)


def near_kernel(*refs):
    for z, ref in enumerate(refs[:-1]):
        refs[-1][z] = ref[1]


def plane_kernel(far, *refs):
    came_ref, out_refs = refs[far], refs[far + 1 :]
    for m, out_ref in enumerate(out_refs):
        for z in range(far):
            out_ref[0, z] = refs[z][0, m]
            out_ref[1, z] = came_ref[z, m]


SUMS = ("00", "01", "10", "r11", "l11")
SLOTS = {"o": ("10", "01"), "d": ("s00", "s11", "t00", "t11")}


def left_kernel(kinds, spots, device_ref, *refs):
    self_refs, left_ref, block_scr = refs[:-2], refs[-2], refs[-1]
    count, momenta, _, orbs, rows2, half = block_scr.shape
    rows = rows2 // 2
    here = device_ref[0]
    me = here % orbs
    collect(block_scr, here, self_refs, spots)
    row, col = grid_masks(half)
    lower, upper = row >= col, row < col
    for k in range(momenta):
        for turn in range(orbs):
            c = me ^ turn
            for part in range(2):
                sheets = {}
                piece = block_scr[:, k, part, c].astype(F32)
                for index in range(2):
                    sheet = jnp.concatenate([piece[d, index * rows : (index + 1) * rows] for d in range(count)], 0)
                    for n, kind in enumerate(kinds):
                        sheets[index, kind] = sheet[n * half : (n + 1) * half]
                pieces = []
                if "o" in kinds:
                    pieces += [sheets[1, "o"].T, sheets[0, "o"]]
                if "d" in kinds:
                    own, facing = sheets[0, "d"], sheets[1, "d"].T
                    pieces += [
                        jnp.where(lower, own, 0.0),
                        jnp.where(lower, facing, 0.0),
                        jnp.where(upper, facing, 0.0),
                        jnp.where(upper, own, 0.0),
                    ]
                at = slice(turn * half, (turn + 1) * half)
                for n, piece in enumerate(pieces):
                    left_ref[k, (2 * n + part) * half : (2 * n + part + 1) * half, at] = piece.astype(BF16)


def langreth_kernel(kinds, sums_in, sums_out, device_ref, left_ref, *refs):
    if sums_in:
        sums_ref, green_scr, out_ref = refs
    else:
        out_ref, green_scr, sems = refs[-3:]
    held, orbs = green_scr.shape[:2]
    momenta, half = green_scr.shape[-3:-1]
    copies = []
    if not sums_in:
        copies = [
            pltpu.make_async_copy(green_any, green_scr.at[n // orbs, n % orbs], sems.at[n])
            for n, green_any in enumerate(refs[:-3])
        ]
    for copy in copies:
        copy.start()
    me = device_ref[0] % orbs
    row, col = grid_masks(half)
    lower, upper = row >= col, row < col
    keep = {1: lower.astype(F32).astype(BF16), -1: upper.astype(F32).astype(BF16)}
    scale = (2 * half) ** -0.5
    blocks = ((0, 0), (0, 1), (1, 0), (1, 1))
    slots = sum((SLOTS[kind] for kind in kinds), ())
    for k in range(momenta):
        if k == 0:
            for copy in copies:
                copy.wait()
        for turn_b in range(orbs):
            b = me ^ turn_b

            def block(turn, pair, part, i, j, mask):
                kind, n = (int(i == j), i) if held == 2 else (0, (i == j) * 2 + i)
                piece = green_scr[kind, turn, part * orbs + pair, n, k]
                return piece * keep[mask] if mask else piece

            def left(slot):
                n = slots.index(slot)
                return left_ref[k, 2 * n * half : 2 * (n + 1) * half, :]

            def plain(slot, i, j, mask):
                right = jnp.concatenate(
                    [
                        jnp.concatenate([block(turn, b, part, i, j, mask) for part in range(2)], 1)
                        for turn in range(orbs)
                    ],
                    0,
                )
                product = jnp.dot(left(slot), right, preferred_element_type=F32)
                real, imag = product[:half], product[half:]
                return real[:, :half] - imag[:, half:], real[:, half:] + imag[:, :half]

            def adjoint(slot, i, j, mask):
                right = jnp.concatenate(
                    [
                        jnp.concatenate([block(turn_b, me ^ turn, part, i, j, mask) for part in range(2)], 0)
                        for turn in range(orbs)
                    ],
                    1,
                )
                product = lax.dot_general(
                    left(slot), right, (((1,), (1,)), ((), ())), preferred_element_type=F32
                )
                real, imag = product[:half], product[half:]
                return real[:, :half] + imag[:, half:], imag[:, :half] - real[:, half:]

            def total_of(*terms):
                return tuple(sum(term[part] for term in terms) for part in range(2))

            terms = {name: [] for name in SUMS}
            if sums_in:
                for n, name in enumerate(SUMS):
                    terms[name].append(tuple(sums_ref[n, part, k, b] for part in range(2)))
            if "o" in kinds:
                terms["01"].append(adjoint("01", 1, 1, 1))
                terms["10"].append(plain("10", 0, 0, 1))
                terms["l11"].append(plain("10", 0, 1, 0))
            if "d" in kinds:
                retarded = plain("s00", 0, 0, 1)
                lesser = total_of(plain("s00", 0, 0, -1), adjoint("t00", 0, 0, 1))
                terms["00"].append(tuple(jnp.where(lower, r, l) for r, l in zip(retarded, lesser)))
                terms["01"] += [plain("s00", 0, 1, 0), adjoint("t00", 1, 0, 0)]
                terms["10"].append(plain("s11", 1, 0, 0))
                terms["r11"].append(plain("s11", 1, 1, 1))
                terms["l11"] += [plain("s11", 1, 1, -1), adjoint("t11", 1, 1, 1)]
            got = {name: total_of(*terms[name]) for name in SUMS}
            if sums_out:
                for n, name in enumerate(SUMS):
                    for part in range(2):
                        out_ref[n, part, k, b] = got[name][part]
                continue
            for part in range(2):
                results = (
                    got["00"][part],
                    got["01"][part],
                    got["10"][part],
                    jnp.where(lower, got["r11"][part], got["l11"][part]),
                )
                for (i, j), result in zip(blocks, results):
                    out_ref[part, k, b, i * half : (i + 1) * half, j * half : (j + 1) * half] = (
                        result * scale
                    ).astype(BF16)


def exchange(axes, count, sent):
    def shift(x, mask):
        return lax.ppermute(x, axes, [(i, i ^ mask) for i in range(count)])

    far, planes, block = len(sent), sent[0].shape[1], sent[0].shape[2:]
    far_sent = [shift(x, 2 * planes * z) if z else x for z, x in enumerate(sent)]
    swap = pl.pallas_call(
        near_kernel,
        out_shape=jax.ShapeDtypeStruct((far, planes) + block, BF16),
        in_specs=[VMEM] * far,
        out_specs=VMEM,
        compiler_params=limit(4),
        name="near",
    )(*far_sent)
    came = shift(swap, 1)
    joined = pl.pallas_call(
        functools.partial(plane_kernel, far),
        out_shape=[jax.ShapeDtypeStruct((2, far) + block, BF16)] * planes,
        in_specs=[VMEM] * (far + 1),
        out_specs=[VMEM] * planes,
        compiler_params=limit(4),
        name="plane",
    )(*far_sent, came)
    return [shift(x, 2 * m) if m else x for m, x in enumerate(joined)]


def gather(orbs, raw):
    held = {0: raw}
    bit = orbs // 2
    while bit:
        swap = [(i, i ^ bit) for i in range(orbs)]
        for turn, piece in list(held.items()):
            held[turn ^ bit] = lax.ppermute(piece, "orb", swap)
        bit //= 2
    return [held[turn] for turn in range(orbs)]


def local(wide, orbs, green, bubble_weight, tile_owner, pairing):
    parts, momenta, pairs, times, _ = green.shape
    all_pairs = bubble_weight.shape[0]
    half = times // 2
    count = wide * orbs
    chunks = 2 if half % count == 0 else 1
    rows2 = 2 * times // count // chunks
    axes = ("wide", "orb")
    planes = min(4, count // 2)
    far = count // (2 * planes)
    block = (momenta, parts, pairs, rows2, half)
    device = lax.axis_index(axes).astype(jnp.int32).reshape(1)
    spread = jnp.kron(bubble_weight, jnp.eye(rows2, dtype=F32)).astype(BF16)
    width = parts * momenta * wide * half

    off, on = ((0, 1), (1, 0)), ((0, 0), (1, 1))
    if chunks == 2:
        plan = [("d", on, 0, True, False), ("o", off, None, False, True)]
    else:
        plan = [("o", off + on, -half, False, False)]
    returned, greens, came_spots = {}, {}, {}

    def sheets(staged):
        if staged:
            return [jax.ShapeDtypeStruct((2, planes) + block, BF16)] * far
        return [jax.ShapeDtypeStruct((count,) + block, BF16)]

    def deliver(staged, sent):
        if staged:
            return exchange(axes, count, sent)
        return [lax.all_to_all(sent[0], axes, 0, 0, tiled=True)]

    def spots(staged, sent):
        return places(count, 2 * planes, sent) if staged else None

    for tag, blocks, start, staged, staged_back in plan:
        came_spots[tag] = spots(staged_back, False)
        raw, *sent = pl.pallas_call(
            functools.partial(pack_kernel, blocks, spots(staged, True)),
            out_shape=[jax.ShapeDtypeStruct((parts * pairs, len(blocks), momenta, half, half), BF16)]
            + sheets(staged),
            in_specs=[SMEM, VMEM],
            out_specs=[VMEM] * (1 + len(sheets(staged))),
            scratch_shapes=[pltpu.VMEM((count,) + block, BF16)],
            compiler_params=limit(8),
        )(device, green)
        greens[tag] = gather(orbs, raw)
        arrived = deliver(staged, sent)
        sent = pl.pallas_call(
            functools.partial(middle_kernel, start, spots(staged, False), spots(staged_back, True)),
            out_shape=sheets(staged_back),
            in_specs=[SMEM] + [VMEM] * (1 + len(arrived)),
            out_specs=[VMEM] * len(sheets(staged_back)),
            scratch_shapes=[pltpu.VMEM((all_pairs, rows2, width), F32)] * 2 + [pltpu.VMEM((count,) + block, BF16)],
            compiler_params=limit(16),
        )(device, spread, *arrived)
        returned[tag] = deliver(staged_back, sent)

    raws = sum((greens[tag] for tag in sorted(greens, reverse=True)), [])
    sums_shape = jax.ShapeDtypeStruct((len(SUMS), parts, momenta, pairs, half, half), F32)
    final = jax.ShapeDtypeStruct(green.shape, BF16)

    held = jax.ShapeDtypeStruct((chunks, orbs) + raws[0].shape, BF16)

    def left(kinds, tag):
        slots = sum(len(SLOTS[kind]) for kind in kinds)
        return pl.pallas_call(
            functools.partial(left_kernel, kinds, came_spots[tag]),
            out_shape=jax.ShapeDtypeStruct((momenta, 2 * slots * half, orbs * half), BF16),
            in_specs=[SMEM] + [VMEM] * len(returned[tag]),
            out_specs=VMEM,
            scratch_shapes=[pltpu.VMEM((count,) + block, BF16)],
            compiler_params=limit(16),
        )(device, *returned[tag])

    def langreth(kinds, tag, sums, out_shape):
        return pl.pallas_call(
            functools.partial(langreth_kernel, kinds, len(sums) > 0, out_shape is sums_shape),
            out_shape=out_shape if sums else [out_shape, held],
            in_specs=[SMEM] + [VMEM] * (1 + len(sums)) + [HBM] * (0 if sums else len(raws)),
            out_specs=VMEM if sums else [VMEM, VMEM],
            scratch_shapes=[] if sums else [pltpu.SemaphoreType.DMA((len(raws),))],
            compiler_params=limit(20),
            name="langreth",
        )(device, left(kinds, tag), *sums, *([] if sums else raws))

    if chunks == 1:
        return langreth(("o", "d"), "o", [], final)[0]
    sums = langreth(("d",), "d", [], sums_shape)
    return langreth(("o",), "o", sums, final)


def solution(mesh):
    return jax.shard_map(
        functools.partial(local, mesh.shape["wide"], mesh.shape["orb"]),
        mesh=mesh,
        in_specs=(P(None, "wide", "orb", None, None), P(), P(), P()),
        out_specs=P(None, "wide", "orb", None, None),
        check_vma=False,
    )
```
